32 devices in a mesh: island: 2 (over x), row: 4 (over z), col: 4 (over y, core).
Axes of the slice: x: 2, y: 2, z: 4, core: 2. Of those that a mesh axis runs over, the one named last changes fastest.
Arguments:
- weights: float32 [2, 4096, 4096], P('island', 'row', 'col'), may hold values from -6 to 6
- bases: float32 [2, 32, 4096], P(None, None, 'col'), may hold values from -0.09375 to 0.09375
- pairs: int32 [2, 1, 2], replicated, may hold values from 0 to 1, as said below
Outputs:
- updated: float32 [2, 4096, 4096], P('island', 'row', 'col')
The draws below stay inside these ranges and needn't reach their ends.
Inputs may be any that keep to these rules, and one draw needn't show every extreme that they name: In each matching every island appears exactly once among the pairs, so each matching is a perfect matching of the 2 islands.
All inputs are finite; a program needn't handle non-finite values.
Results may differ from the reference program's by a relative error of at most 0.00011.
Values sent between devices are 32-bit elements; how exact they have to be, the bound alone decides.
No kernel may reach another device: no remote copies, remote signals or barrier semaphores. Data moves between devices by JAX's collectives and lax.ppermute only.
A program may use at most 64 MiB of HBM per device.

```python
import jax
import jax.numpy as jnp
from jax import lax

D = 4096
RANK = 32
MATCHINGS = 2
COLS = 4096
ISLANDS = 2


def draw_pairs(key, part):
    listing = []
    half = ISLANDS // 2
    for matching in range(MATCHINGS):
        sub = jax.random.fold_in(key, 7 + matching)
        anchor = jax.random.randint(jax.random.fold_in(sub, 1), (), 0, ISLANDS).astype(jnp.int32)
        across = ((anchor + half) % ISLANDS).astype(jnp.int32)
        ranks = jnp.argsort(jax.random.permutation(jax.random.fold_in(sub, 2), ISLANDS)).astype(jnp.int32)
        ranks = ranks.at[anchor].set(-2).at[across].set(-1)
        order = jnp.argsort(ranks, stable=True).astype(jnp.int32)
        paired = order.reshape(half, 2)
        shuffle = jax.random.permutation(jax.random.fold_in(sub, 3), half).astype(jnp.int32)
        paired = paired[shuffle]
        flips = jax.random.randint(jax.random.fold_in(sub, 4), (half,), 0, 2).astype(jnp.int32)
        first = jnp.where(flips == 1, paired[:, 1], paired[:, 0])
        second = jnp.where(flips == 1, paired[:, 0], paired[:, 1])
        listing.append(jnp.stack([first, second], axis=1).astype(jnp.int32))
    return jnp.stack(listing).astype(jnp.int32)


def steps_of(rng, shape, shards, smallest, top_value):
    factor_of, own = 1.0, jax.random.fold_in(rng, 6)
    for position, shards_of in shards:
        steps = jnp.exp(jax.random.uniform(jax.random.fold_in(own, position), (shards_of,), jnp.float32, smallest / len(shards), top_value / len(shards)))
        factor_of = factor_of * jnp.repeat(steps, shape[position] // shards_of).reshape([-1 if axis == position else 1 for axis in range(len(shape))])
    return factor_of


def noise(own_key, shape, deviation, limit, cuts=(), kind=jnp.bfloat16):
    result = jax.random.normal(own_key, shape, jnp.float32) * deviation
    if len(cuts) > 0:
        result = steps_of(own_key, shape, cuts, -0.22, 0.18) * result
    return jnp.clip(result, min=-limit, max=limit).astype(kind)


def setup_inputs(seed: int = 0) -> dict:
    arg_keys = jax.random.split(jax.random.key(seed), 4)
    return {
        "weights": noise(arg_keys[0], (ISLANDS, D, COLS), 1.0, 6.0, ((0, 2), (1, 4), (2, 4)), jnp.float32),
        "bases": noise(arg_keys[1], (MATCHINGS, RANK, COLS), COLS ** -0.5, 0.09375, ((2, 4),), jnp.float32),
        "pairs": draw_pairs(jax.random.fold_in(arg_keys[3], 71), 0),
    }


def partner_list(pair_rows, islands):
    positions = jnp.arange(islands, dtype=jnp.int32)
    first = pair_rows[:, 0].astype(jnp.int32)
    second = pair_rows[:, 1].astype(jnp.int32)
    from_first = jnp.where(first[None, :] == positions[:, None], second[None, :], 0)
    from_second = jnp.where(second[None, :] == positions[:, None], first[None, :], 0)
    return jnp.sum(from_first + from_second, axis=1).astype(jnp.int32)

def orthonormal(left_factor):
    gram_matrix = jnp.dot(left_factor, left_factor.T, precision=lax.Precision.HIGHEST)
    lower_factor = jnp.linalg.cholesky(gram_matrix)
    return jax.scipy.linalg.solve_triangular(lower_factor, left_factor, lower=True)

def reference(weights, bases, pairs):
    current = weights
    for matching in range(MATCHINGS):
        partner_row = partner_list(pairs[matching], ISLANDS)
        left_terms = jnp.einsum('rc,idc->ird', bases[matching], current, precision=lax.Precision.HIGHEST)
        left_factor = left_terms - jnp.take(left_terms, partner_row, axis=0)
        left_basis = jax.vmap(orthonormal)(left_factor)
        right_terms = jnp.einsum('ird,idc->irc', left_basis, current, precision=lax.Precision.HIGHEST)
        right_factor = right_terms + jnp.take(right_terms, partner_row, axis=0)
        current = current - 0.5 * jnp.einsum('ird,irc->idc', left_basis, right_factor, precision=lax.Precision.HIGHEST)
    return current
```

```python
import jax
import jax.numpy as jnp
from jax import lax
from jax.sharding import PartitionSpec as P

MATCHINGS = 2
AXES = ("island", "row", "col")


def partner_list(pair_rows, islands):
    positions = jnp.arange(islands, dtype=jnp.int32)
    first = pair_rows[:, 0]
    second = pair_rows[:, 1]
    from_first = jnp.where(first[None, :] == positions[:, None], second[None, :], 0)
    from_second = jnp.where(second[None, :] == positions[:, None], first[None, :], 0)
    return jnp.sum(from_first + from_second, axis=1)


def orthonormal(gram_matrix, left_factor):
    lower_factor = jnp.linalg.cholesky(gram_matrix)
    return jax.scipy.linalg.solve_triangular(lower_factor, left_factor, lower=True)


def combine_partner(values, partner_row, myself, factor_sign):
    islands = lax.axis_size("island")
    gathered = lax.all_gather(values[None], "island", axis=0, tiled=True)
    positions = jnp.arange(islands, dtype=jnp.int32)
    mine = jnp.sum(jnp.where(positions == myself, partner_row, 0))
    partner_term = lax.dynamic_index_in_dim(gathered, mine, 0, keepdims=False)
    return values + factor_sign * partner_term


def any_islands(weights, bases, pairs):
    myself = lax.axis_index("island")
    islands = lax.axis_size("island")
    weight_tile = weights[0]
    for matching in range(MATCHINGS):
        base_rows = bases[matching]
        partner_row = partner_list(pairs[matching], islands)
        partial_terms = lax.dot_general(
            base_rows,
            weight_tile,
            (((1,), (1,)), ((), ())),
            precision=lax.Precision.HIGHEST,
            preferred_element_type=jnp.float32,
        )
        left_terms = lax.psum(partial_terms, "col")
        left_factor = combine_partner(left_terms, partner_row, myself, -1.0)
        local_gram = jnp.dot(left_factor, left_factor.T, precision=lax.Precision.HIGHEST)
        gram_matrix = lax.psum(local_gram, "row")
        left_basis = orthonormal(gram_matrix, left_factor)
        right_partial = jnp.dot(left_basis, weight_tile, precision=lax.Precision.HIGHEST)
        right_terms = lax.psum(right_partial, "row")
        right_factor = combine_partner(right_terms, partner_row, myself, 1.0)
        correction = lax.dot_general(
            left_basis,
            right_factor,
            (((0,), (0,)), ((), ())),
            precision=lax.Precision.HIGHEST,
            preferred_element_type=jnp.float32,
        )
        weight_tile = weight_tile - 0.5 * correction
    return weight_tile[None]


def exchange(values, island=0, row=0, col=0):
    sizes = [lax.axis_size(axis) for axis in AXES]
    pairs = []
    for i in range(sizes[0]):
        for r in range(sizes[1]):
            for c in range(sizes[2]):
                here = (i * sizes[1] + r) * sizes[2] + c
                there = ((i ^ island) * sizes[1] + (r ^ row)) * sizes[2] + (c ^ col)
                pairs.append((here, there))
    return lax.ppermute(values, AXES, pairs)


def two_islands(weights, bases, pairs):
    del pairs
    island = lax.axis_index("island")
    row = lax.axis_index("row")
    col = lax.axis_index("col")
    sign = jnp.where(island == 0, 1.0, -1.0).astype(jnp.float32)
    tile = weights[0]
    rows, cols = tile.shape
    stacked = bases.reshape(-1, cols) * sign
    count = stacked.shape[0]

    partial = lax.dot_general(stacked, tile, (((1,), (1,)), ((), ())), precision=lax.Precision.HIGH, preferred_element_type=jnp.float32)
    core = col % 2
    halves = partial.reshape(count, 2, rows // 2).transpose(1, 0, 2)
    mine = lax.dynamic_index_in_dim(halves, core, 0, keepdims=False)
    other = lax.dynamic_index_in_dim(halves, 1 - core, 0, keepdims=False)
    mine = mine + exchange(other, col=1)
    mine = mine + exchange(mine, island=1) + exchange(mine, col=2) + exchange(mine, island=1, col=2)
    other = exchange(mine, col=1)
    factor = jnp.where(core == 0, jnp.concatenate([mine, other], axis=1), jnp.concatenate([other, mine], axis=1))

    gram = lax.dot_general(factor, factor, (((1,), (1,)), ((), ())), precision=lax.Precision.HIGHEST, preferred_element_type=jnp.float32)
    product = jnp.dot(factor * sign, tile, precision=lax.Precision.HIGH, preferred_element_type=jnp.float32)
    place = island * 2 + row % 2
    blocks = product.reshape(count, 4, cols // 4).transpose(1, 0, 2)
    block = [lax.dynamic_index_in_dim(blocks, place ^ k, 0, keepdims=False) for k in range(4)]
    width = cols // 4
    with_gram = exchange(jnp.concatenate([block[1], gram], axis=1), row=1)
    total = block[0] + exchange(block[2], island=1) + exchange(block[3], island=1, row=1) + with_gram[:, :width]
    gram = gram + with_gram[:, width:]
    both = jnp.concatenate([total, gram], axis=1)
    both = both + exchange(both, row=2)
    total, gram = both[:, :width], both[:, width:]
    parts = [total, exchange(total, row=1), exchange(total, island=1), exchange(total, island=1, row=1)]
    lower = jnp.linalg.cholesky(gram)
    basis = jax.scipy.linalg.solve_triangular(lower, factor, lower=True)
    stack = jnp.stack(parts)
    right = jnp.concatenate([lax.dynamic_index_in_dim(stack, place ^ k, 0, keepdims=False) for k in range(4)], axis=1)
    right = jax.scipy.linalg.solve_triangular(lower, right, lower=True)
    correction = lax.dot_general(basis * (0.5 * sign), right, (((0,), (0,)), ((), ())), precision=lax.Precision.HIGH, preferred_element_type=jnp.float32)
    return (tile - correction)[None]


def solution(mesh):
    in_specs = (P("island", "row", "col"), P(None, None, "col"), P())
    out_specs = P("island", "row", "col")
    sizes = tuple(mesh.shape[axis] for axis in AXES)
    body = two_islands if sizes == (2, 4, 4) else any_islands
    return jax.shard_map(body, mesh=mesh, in_specs=in_specs, out_specs=out_specs, check_vma=False)
```

```python
import jax
import jax.numpy as jnp
from jax import lax
from jax.experimental import pallas as pl
from jax.experimental.pallas import tpu as pltpu
from jax.sharding import PartitionSpec as P

MATCHINGS = 2
AXES = ("island", "row", "col")


def partner_list(pair_rows, islands):
    positions = jnp.arange(islands, dtype=jnp.int32)
    first = pair_rows[:, 0]
    second = pair_rows[:, 1]
    from_first = jnp.where(first[None, :] == positions[:, None], second[None, :], 0)
    from_second = jnp.where(second[None, :] == positions[:, None], first[None, :], 0)
    return jnp.sum(from_first + from_second, axis=1)


def orthonormal(gram_matrix, left_factor):
    lower_factor = jnp.linalg.cholesky(gram_matrix)
    return jax.scipy.linalg.solve_triangular(lower_factor, left_factor, lower=True)


def combine_partner(values, partner_row, myself, factor_sign):
    islands = lax.axis_size("island")
    gathered = lax.all_gather(values[None], "island", axis=0, tiled=True)
    positions = jnp.arange(islands, dtype=jnp.int32)
    mine = jnp.sum(jnp.where(positions == myself, partner_row, 0))
    partner_term = lax.dynamic_index_in_dim(gathered, mine, 0, keepdims=False)
    return values + factor_sign * partner_term


def any_islands(weights, bases, pairs):
    myself = lax.axis_index("island")
    islands = lax.axis_size("island")
    weight_tile = weights[0]
    for matching in range(MATCHINGS):
        base_rows = bases[matching]
        partner_row = partner_list(pairs[matching], islands)
        partial_terms = lax.dot_general(
            base_rows,
            weight_tile,
            (((1,), (1,)), ((), ())),
            precision=lax.Precision.HIGHEST,
            preferred_element_type=jnp.float32,
        )
        left_terms = lax.psum(partial_terms, "col")
        left_factor = combine_partner(left_terms, partner_row, myself, -1.0)
        local_gram = jnp.dot(left_factor, left_factor.T, precision=lax.Precision.HIGHEST)
        gram_matrix = lax.psum(local_gram, "row")
        left_basis = orthonormal(gram_matrix, left_factor)
        right_partial = jnp.dot(left_basis, weight_tile, precision=lax.Precision.HIGHEST)
        right_terms = lax.psum(right_partial, "row")
        right_factor = combine_partner(right_terms, partner_row, myself, 1.0)
        correction = lax.dot_general(
            left_basis,
            right_factor,
            (((0,), (0,)), ((), ())),
            precision=lax.Precision.HIGHEST,
            preferred_element_type=jnp.float32,
        )
        weight_tile = weight_tile - 0.5 * correction
    return weight_tile[None]


def exchange(values, island=0, row=0, col=0):
    sizes = [lax.axis_size(axis) for axis in AXES]
    pairs = []
    for i in range(sizes[0]):
        for r in range(sizes[1]):
            for c in range(sizes[2]):
                here = (i * sizes[1] + r) * sizes[2] + c
                there = ((i ^ island) * sizes[1] + (r ^ row)) * sizes[2] + (c ^ col)
                pairs.append((here, there))
    return lax.ppermute(values, AXES, pairs)


def split(values):
    high = values.astype(jnp.bfloat16)
    return high, (values - high.astype(jnp.float32)).astype(jnp.bfloat16)


def matmul(left, right, contract):
    return lax.dot_general(left, right, (contract, ((), ())), preferred_element_type=jnp.float32)


def island_sign():
    return jnp.where(lax.axis_index("island") == 0, 1.0, -1.0).astype(jnp.float32)


def left_kernel(tile_ref, bases_ref, kept_ref, other_ref, mine_ref, rows_buffer, rows_sem, sems):
    rows, cols = tile_ref.shape
    core = lax.rem(lax.axis_index("col"), 2)
    blocks = sems.shape[0]
    size = rows // blocks
    spans = []
    for block in range(blocks):
        half = 1 - core if block < blocks // 2 else core
        spans.append(pl.ds(pl.multiple_of(half * (rows // 2) + block % (blocks // 2) * size, size), size))
    copies = [pltpu.make_async_copy(tile_ref.at[span, :], kept_ref.at[span, :], sems.at[block]) for block, span in enumerate(spans)]
    rows_copy = pltpu.make_async_copy(bases_ref, rows_buffer, rows_sem)
    rows_copy.start()
    for copy in copies:
        copy.start()
    rows_copy.wait()
    stacked = rows_buffer[...].reshape(-1, cols) * island_sign()
    count = stacked.shape[0]
    high, low = split(stacked)
    both = jnp.concatenate([high, low], axis=0)
    for block in range(blocks):
        copies[block].wait()
        tile_high, tile_low = split(kept_ref[spans[block], :])
        first = matmul(both, tile_high, ((1,), (1,)))
        second = matmul(high, tile_low, ((1,), (1,)))
        out_ref = other_ref if block < blocks // 2 else mine_ref
        start = block % (blocks // 2) * size
        out_ref[:, start : start + size] = first[:count] + first[count:] + second


def right_kernel(tile_ref, mine_ref, other_ref, out0_ref, out1_ref, out2_ref, out3_ref, factor):
    rows, cols = tile_ref.shape
    width = cols // 4
    half = rows // 2
    core = lax.rem(lax.axis_index("col"), 2)
    place = lax.axis_index("island") * 2 + lax.rem(lax.axis_index("row"), 2)
    factor[:, pl.ds(pl.multiple_of(core * half, half), half)] = mine_ref[...]
    factor[:, pl.ds(pl.multiple_of((1 - core) * half, half), half)] = other_ref[...]
    values = factor[...]
    count = values.shape[0]
    gram = lax.dot_general(values, values, (((1,), (1,)), ((), ())), precision=lax.Precision.HIGHEST, preferred_element_type=jnp.float32)
    quarter = count // 4
    packed = jnp.concatenate([gram[i * quarter : (i + 1) * quarter, :] for i in range(4)], axis=1)
    out0_ref[count:, :] = packed
    out1_ref[count:, :] = packed
    high, low = split(values * island_sign())
    both = jnp.concatenate([high, low], axis=0)
    for block, out_ref in enumerate((out0_ref, out1_ref, out2_ref, out3_ref)):
        start = pl.multiple_of(lax.bitwise_xor(place, block) * width, width)
        tile_high, tile_low = split(tile_ref[:, pl.ds(start, width)])
        first = matmul(both, tile_high, ((1,), (0,)))
        second = matmul(high, tile_low, ((1,), (0,)))
        out_ref[:count, :] = first[:count] + first[count:] + second


def add_kernel(own_ref, near_ref, across_ref, both_ref, out_ref):
    count = across_ref.shape[0]
    out_ref[:count, :] = own_ref[:count, :] + near_ref[:count, :] + across_ref[...] + both_ref[...]
    out_ref[count:, :] = own_ref[count:, :] + near_ref[count:, :]


def finish_kernel(own_ref, far_ref, total_ref, gram_ref):
    count = total_ref.shape[0]
    total_ref[...] = own_ref[:count, :] + far_ref[:count, :]
    gram_ref[...] = own_ref[count:, :] + far_ref[count:, :]


def inverse_kernel(packed_ref, mine_ref, other_ref, out_ref, factor):
    packed = packed_ref[...]
    quarter = packed.shape[0]
    count = 4 * quarter
    half = mine_ref.shape[1]
    core = lax.rem(lax.axis_index("col"), 2)
    factor[:, pl.ds(pl.multiple_of(core * half, half), half)] = mine_ref[...]
    factor[:, pl.ds(pl.multiple_of((1 - core) * half, half), half)] = other_ref[...]
    matrix = jnp.concatenate([packed[:, i * count : (i + 1) * count] for i in range(4)], axis=0)
    row_index = lax.broadcasted_iota(jnp.int32, (count, count), 0)
    col_index = lax.broadcasted_iota(jnp.int32, (count, count), 1)
    panel = 8
    for first in range(0, count, panel):
        columns = [jnp.broadcast_to(matrix[:, first + k : first + k + 1], (count, count)) for k in range(panel)]
        for k in range(panel):
            pivot = first + k
            inverse = 1.0 / columns[k][pivot : pivot + 1, :]
            scaled = matrix[pivot : pivot + 1, :] * inverse
            in_row = row_index == pivot
            matrix = jnp.where(in_row, scaled, matrix - columns[k] * scaled)
            matrix = jnp.where(col_index == pivot, jnp.where(in_row, -inverse, columns[k] * inverse), matrix)
            for later in range(k + 1, panel):
                entry = columns[later][pivot : pivot + 1, :] * inverse
                columns[later] = jnp.where(in_row, entry, columns[later] - columns[k] * entry)
    scaled = matrix * (-0.5 * island_sign())
    right = lax.dot_general(scaled, factor[...], (((0,), (0,)), ((), ())), precision=lax.Precision.HIGHEST, preferred_element_type=jnp.float32)
    high, low = split(right.T)
    out_ref[...] = jnp.concatenate([high, high, low], axis=1)


def update_kernel(tile_ref, left_ref, right0_ref, right1_ref, right2_ref, right3_ref, out_ref, results, sems):
    rows, cols = tile_ref.shape
    width = cols // 4
    place = lax.axis_index("island") * 2 + lax.rem(lax.axis_index("row"), 2)
    spans = [pl.ds(pl.multiple_of(lax.bitwise_xor(place, k) * width, width), width) for k in range(4)]
    stores = [pltpu.make_async_copy(results.at[k], out_ref.at[:, spans[k]], sems.at[k]) for k in range(4)]
    left = left_ref[...]
    for k, right_ref in enumerate((right0_ref, right1_ref, right2_ref, right3_ref)):
        high, low = split(right_ref[...])
        correction = matmul(left, jnp.concatenate([high, low, high], axis=0), ((1,), (0,)))
        results[k] = tile_ref[:, spans[k]] - correction
        stores[k].start()
    for store in stores:
        store.wait()


def in_vmem(count):
    return [pl.BlockSpec(memory_space=pltpu.VMEM)] * count


def grant(mebibytes):
    return pltpu.CompilerParams(vmem_limit_bytes=mebibytes << 20)


def two_islands(weights, bases, pairs):
    del pairs
    tile = weights[0]
    rows, cols = tile.shape
    count = bases.shape[0] * bases.shape[1]
    width = cols // 4
    extra = count // 4
    f32 = jnp.float32
    anywhere = pl.BlockSpec(memory_space=pl.ANY)
    half_shape = jax.ShapeDtypeStruct((count, rows // 2), f32)
    block_shape = jax.ShapeDtypeStruct((count, width), f32)
    long_shape = jax.ShapeDtypeStruct((count + extra, width), f32)

    kept, other, mine = pl.pallas_call(
        left_kernel,
        out_shape=(jax.ShapeDtypeStruct((rows, cols), f32), half_shape, half_shape),
        in_specs=[anywhere] * 2,
        out_specs=in_vmem(3),
        scratch_shapes=[pltpu.VMEM(bases.shape, f32), pltpu.SemaphoreType.DMA(()), pltpu.SemaphoreType.DMA((8,))],
        compiler_params=grant(8),
        name="left",
    )(pltpu.with_memory_space_constraint(tile, pltpu.HBM), pltpu.with_memory_space_constraint(bases, pltpu.HBM))
    mine = mine + exchange(other, col=1)
    mine = mine + exchange(mine, island=1) + exchange(mine, col=2) + exchange(mine, island=1, col=2)
    other = exchange(mine, col=1)

    block0, block1, block2, block3 = pl.pallas_call(
        right_kernel,
        out_shape=(long_shape, long_shape, block_shape, block_shape),
        in_specs=in_vmem(3),
        out_specs=in_vmem(4),
        scratch_shapes=[pltpu.VMEM((count, rows), f32)],
        compiler_params=grant(10),
        name="right",
    )(kept, mine, other)
    summed = pl.pallas_call(add_kernel, out_shape=long_shape, in_specs=in_vmem(4), out_specs=in_vmem(1)[0], compiler_params=grant(2), name="add")(
        block0, exchange(block1, row=1), exchange(block2, island=1), exchange(block3, island=1, row=1)
    )
    total, gram = pl.pallas_call(
        finish_kernel,
        out_shape=(block_shape, jax.ShapeDtypeStruct((extra, width), f32)),
        in_specs=in_vmem(2),
        out_specs=in_vmem(2),
        compiler_params=grant(2),
        name="finish",
    )(summed, exchange(summed, row=2))
    rights = [total, exchange(total, row=1), exchange(total, island=1), exchange(total, island=1, row=1)]
    left = pl.pallas_call(
        inverse_kernel,
        out_shape=jax.ShapeDtypeStruct((rows, 3 * count), jnp.bfloat16),
        in_specs=in_vmem(3),
        out_specs=in_vmem(1)[0],
        scratch_shapes=[pltpu.VMEM((count, rows), f32)],
        cost_estimate=pl.CostEstimate(flops=100_000_000, bytes_accessed=4_000_000, transcendentals=0),
        compiler_params=grant(6),
        name="inverse",
    )(gram, mine, other)
    updated = pl.pallas_call(
        update_kernel,
        out_shape=jax.ShapeDtypeStruct((rows, cols), f32),
        in_specs=in_vmem(6),
        out_specs=anywhere,
        scratch_shapes=[pltpu.VMEM((4, rows, width), f32), pltpu.SemaphoreType.DMA((4,))],
        compiler_params=grant(14),
        name="update",
    )(kept, left, *rights)
    return updated[None]


def solution(mesh):
    in_specs = (P("island", "row", "col"), P(None, None, "col"), P())
    out_specs = P("island", "row", "col")
    sizes = tuple(mesh.shape[axis] for axis in AXES)
    body = two_islands if sizes == (2, 4, 4) else any_islands
    return jax.shard_map(body, mesh=mesh, in_specs=in_specs, out_specs=out_specs, check_vma=False)
```

```python
import jax
import jax.numpy as jnp
from jax import lax
from jax.experimental import pallas as pl
from jax.experimental.pallas import tpu as pltpu
from jax.sharding import PartitionSpec as P

MATCHINGS = 2
AXES = ("island", "row", "col")


def partner_list(pair_rows, islands):
    positions = jnp.arange(islands, dtype=jnp.int32)
    first = pair_rows[:, 0]
    second = pair_rows[:, 1]
    from_first = jnp.where(first[None, :] == positions[:, None], second[None, :], 0)
    from_second = jnp.where(second[None, :] == positions[:, None], first[None, :], 0)
    return jnp.sum(from_first + from_second, axis=1)


def orthonormal(gram_matrix, left_factor):
    lower_factor = jnp.linalg.cholesky(gram_matrix)
    return jax.scipy.linalg.solve_triangular(lower_factor, left_factor, lower=True)


def combine_partner(values, partner_row, myself, factor_sign):
    islands = lax.axis_size("island")
    gathered = lax.all_gather(values[None], "island", axis=0, tiled=True)
    positions = jnp.arange(islands, dtype=jnp.int32)
    mine = jnp.sum(jnp.where(positions == myself, partner_row, 0))
    partner_term = lax.dynamic_index_in_dim(gathered, mine, 0, keepdims=False)
    return values + factor_sign * partner_term


def any_islands(weights, bases, pairs):
    myself = lax.axis_index("island")
    islands = lax.axis_size("island")
    weight_tile = weights[0]
    for matching in range(MATCHINGS):
        base_rows = bases[matching]
        partner_row = partner_list(pairs[matching], islands)
        partial_terms = lax.dot_general(
            base_rows,
            weight_tile,
            (((1,), (1,)), ((), ())),
            precision=lax.Precision.HIGHEST,
            preferred_element_type=jnp.float32,
        )
        left_terms = lax.psum(partial_terms, "col")
        left_factor = combine_partner(left_terms, partner_row, myself, -1.0)
        local_gram = jnp.dot(left_factor, left_factor.T, precision=lax.Precision.HIGHEST)
        gram_matrix = lax.psum(local_gram, "row")
        left_basis = orthonormal(gram_matrix, left_factor)
        right_partial = jnp.dot(left_basis, weight_tile, precision=lax.Precision.HIGHEST)
        right_terms = lax.psum(right_partial, "row")
        right_factor = combine_partner(right_terms, partner_row, myself, 1.0)
        correction = lax.dot_general(
            left_basis,
            right_factor,
            (((0,), (0,)), ((), ())),
            precision=lax.Precision.HIGHEST,
            preferred_element_type=jnp.float32,
        )
        weight_tile = weight_tile - 0.5 * correction
    return weight_tile[None]


def exchange(values, island=0, row=0, col=0):
    sizes = [lax.axis_size(axis) for axis in AXES]
    pairs = []
    for i in range(sizes[0]):
        for r in range(sizes[1]):
            for c in range(sizes[2]):
                here = (i * sizes[1] + r) * sizes[2] + c
                there = ((i ^ island) * sizes[1] + (r ^ row)) * sizes[2] + (c ^ col)
                pairs.append((here, there))
    return lax.ppermute(values, AXES, pairs)


def split(values):
    high = values.astype(jnp.bfloat16)
    return high, (values - high.astype(jnp.float32)).astype(jnp.bfloat16)


def matmul(left, right, contract):
    return lax.dot_general(left, right, (contract, ((), ())), preferred_element_type=jnp.float32)


def island_sign():
    return jnp.where(lax.axis_index("island") == 0, 1.0, -1.0).astype(jnp.float32)


def core_halves(rows):
    core = lax.rem(lax.axis_index("col"), 2)
    half = rows // 2
    return pl.multiple_of(core * half, half), pl.multiple_of((1 - core) * half, half)


def left_rows(tile, both, high):
    count = high.shape[0]
    tile_high, tile_low = split(tile)
    first = matmul(tile_high, both, ((1,), (1,)))
    second = matmul(tile_low, high, ((1,), (1,)))
    return (first[:, :count] + first[:, count:] + second).T


def left_kernel(tile_ref, bases_ref, kept_ref, other_ref, first_ref, both_ref, rows_buffer, rows_sem, sems):
    rows, cols = tile_ref.shape
    size = rows // 4
    mine, other = core_halves(rows)
    spans = [pl.ds(start, size) for start in (other, pl.multiple_of(other + size, size), mine, pl.multiple_of(mine + size, size))]
    copies = [pltpu.make_async_copy(tile_ref.at[span, :], kept_ref.at[span, :], sems.at[block]) for block, span in enumerate(spans)]
    rows_copy = pltpu.make_async_copy(bases_ref, rows_buffer, rows_sem)
    rows_copy.start()
    for copy in copies:
        copy.start()
    rows_copy.wait()
    stacked = rows_buffer[...].reshape(-1, cols) * island_sign()
    high, low = split(stacked)
    both = jnp.concatenate([high, low], axis=0)
    both_ref[...] = both
    for block in range(3):
        copies[block].wait()
        values = left_rows(kept_ref[spans[block], :], both, high)
        if block < 2:
            other_ref[:, block * size : (block + 1) * size] = values
        else:
            first_ref[...] = values
    copies[3].wait()


def rest_kernel(tile_ref, first_ref, both_ref, mine_ref):
    rows, cols = tile_ref.shape
    size = rows // 4
    mine, _ = core_halves(rows)
    both = both_ref[...]
    high = both[: both.shape[0] // 2]
    mine_ref[:, :size] = first_ref[...]
    mine_ref[:, size:] = left_rows(tile_ref[pl.ds(pl.multiple_of(mine + size, size), size), :], both, high)


def block_place():
    return lax.axis_index("island") * 2 + lax.rem(lax.axis_index("row"), 2)


def block_spans(width):
    place = block_place()
    return [pl.ds(pl.multiple_of(lax.bitwise_xor(place, k) * width, width), width) for k in range(4)]


def own_right_kernel(tile_ref, mine_ref, out_ref):
    rows, cols = tile_ref.shape
    mine, _ = core_halves(rows)
    values = mine_ref[...]
    count = values.shape[0]
    high, low = split(values * island_sign())
    both = jnp.concatenate([high, low], axis=0)
    for block, span in enumerate(block_spans(cols // 4)):
        tile_high, tile_low = split(tile_ref[pl.ds(mine, rows // 2), span])
        first = matmul(both, tile_high, ((1,), (0,)))
        second = matmul(high, tile_low, ((1,), (0,)))
        out_ref[block] = first[:count] + first[count:] + second


def right_kernel(tile_ref, mine_ref, other_ref, part_ref, out0_ref, out1_ref, out2_ref, out3_ref):
    rows, cols = tile_ref.shape
    _, other = core_halves(rows)
    count = mine_ref.shape[0]
    gram = jnp.zeros((count, count), jnp.float32)
    for part in (mine_ref[...], other_ref[...]):
        gram += lax.dot_general(part, part, (((1,), (1,)), ((), ())), precision=lax.Precision.HIGHEST, preferred_element_type=jnp.float32)
    quarter = count // 4
    packed = jnp.concatenate([gram[i * quarter : (i + 1) * quarter, :] for i in range(4)], axis=1)
    out0_ref[count:, :] = packed
    out1_ref[count:, :] = packed
    high, low = split(other_ref[...] * island_sign())
    both = jnp.concatenate([high, low], axis=0)
    outs = (out0_ref, out1_ref, out2_ref, out3_ref)
    for block, span in enumerate(block_spans(cols // 4)):
        tile_high, tile_low = split(tile_ref[pl.ds(other, rows // 2), span])
        first = matmul(both, tile_high, ((1,), (0,)))
        second = matmul(high, tile_low, ((1,), (0,)))
        outs[block][:count, :] = part_ref[block] + (first[:count] + first[count:] + second)


def add_kernel(own_ref, near_ref, across_ref, both_ref, out_ref):
    count = across_ref.shape[0]
    out_ref[:count, :] = own_ref[:count, :] + near_ref[:count, :] + across_ref[...] + both_ref[...]
    out_ref[count:, :] = own_ref[count:, :] + near_ref[count:, :]


def finish_kernel(own_ref, far_ref, total_ref, gram_ref):
    count = total_ref.shape[0]
    total_ref[...] = own_ref[:count, :] + far_ref[:count, :]
    gram_ref[...] = own_ref[count:, :] + far_ref[count:, :]


def inverse_kernel(packed_ref, mine_ref, other_ref, out_ref, factor):
    packed = packed_ref[...]
    quarter = packed.shape[0]
    count = 4 * quarter
    half = mine_ref.shape[1]
    mine, other = core_halves(2 * half)
    factor[:, pl.ds(mine, half)] = mine_ref[...]
    factor[:, pl.ds(other, half)] = other_ref[...]
    matrix = jnp.concatenate([packed[:, i * count : (i + 1) * count] for i in range(4)], axis=0)
    row_index = lax.broadcasted_iota(jnp.int32, (count, count), 0)
    col_index = lax.broadcasted_iota(jnp.int32, (count, count), 1)
    panel = 8
    for first in range(0, count, panel):
        columns = [jnp.broadcast_to(matrix[:, first + k : first + k + 1], (count, count)) for k in range(panel)]
        for k in range(panel):
            pivot = first + k
            inverse = 1.0 / columns[k][pivot : pivot + 1, :]
            scaled = matrix[pivot : pivot + 1, :] * inverse
            in_row = row_index == pivot
            matrix = jnp.where(in_row, scaled, matrix - columns[k] * scaled)
            matrix = jnp.where(col_index == pivot, jnp.where(in_row, -inverse, columns[k] * inverse), matrix)
            for later in range(k + 1, panel):
                entry = columns[later][pivot : pivot + 1, :] * inverse
                columns[later] = jnp.where(in_row, entry, columns[later] - columns[k] * entry)
    scaled = matrix * (-0.5 * island_sign())
    right = lax.dot_general(scaled, factor[...], (((0,), (0,)), ((), ())), precision=lax.Precision.HIGHEST, preferred_element_type=jnp.float32)
    high, low = split(right.T)
    out_ref[...] = jnp.concatenate([high, high, low], axis=1)


def update_kernel(tile_ref, left_ref, right0_ref, right1_ref, right2_ref, right3_ref, out_ref, results, sems):
    rows, cols = tile_ref.shape
    width = cols // 4
    spans = block_spans(width)
    stores = [pltpu.make_async_copy(results.at[k], out_ref.at[:, spans[k]], sems.at[k]) for k in range(4)]
    left = left_ref[...]
    for k, right_ref in enumerate((right0_ref, right1_ref, right2_ref, right3_ref)):
        high, low = split(right_ref[...])
        correction = matmul(left, jnp.concatenate([high, low, high], axis=0), ((1,), (0,)))
        results[k] = tile_ref[:, spans[k]] - correction
        stores[k].start()
    for store in stores:
        store.wait()


def in_vmem(count):
    return [pl.BlockSpec(memory_space=pltpu.VMEM)] * count


def grant(mebibytes):
    return pltpu.CompilerParams(vmem_limit_bytes=mebibytes << 20)


def work(flops):
    return pl.CostEstimate(flops=flops, bytes_accessed=flops // 32, transcendentals=0)


def two_islands(weights, bases, pairs):
    del pairs
    tile = weights[0]
    rows, cols = tile.shape
    count = bases.shape[0] * bases.shape[1]
    width = cols // 4
    extra = count // 4
    f32 = jnp.float32
    anywhere = pl.BlockSpec(memory_space=pl.ANY)
    half_shape = jax.ShapeDtypeStruct((count, rows // 2), f32)
    block_shape = jax.ShapeDtypeStruct((count, width), f32)
    long_shape = jax.ShapeDtypeStruct((count + extra, width), f32)

    hbm_tile, hbm_bases = (pltpu.with_memory_space_constraint(array, pltpu.HBM) for array in (tile, bases))
    kept, other, first, both = pl.pallas_call(
        left_kernel,
        out_shape=(
            jax.ShapeDtypeStruct((rows, cols), f32),
            half_shape,
            jax.ShapeDtypeStruct((count, rows // 4), f32),
            jax.ShapeDtypeStruct((2 * count, cols), jnp.bfloat16),
        ),
        in_specs=[anywhere] * 2,
        out_specs=in_vmem(4),
        scratch_shapes=[pltpu.VMEM(bases.shape, f32), pltpu.SemaphoreType.DMA(()), pltpu.SemaphoreType.DMA((4,))],
        compiler_params=grant(8),
        name="left",
    )(hbm_tile, hbm_bases)
    crossed = exchange(other, col=1)
    mine = pl.pallas_call(
        rest_kernel,
        out_shape=half_shape,
        in_specs=in_vmem(3),
        out_specs=in_vmem(1)[0],
        compiler_params=grant(6),
        cost_estimate=work(2 * rows // 4 * cols * count),
        name="rest",
    )(kept, first, both)
    mine = mine + crossed
    mine = mine + exchange(mine, island=1) + exchange(mine, col=2) + exchange(mine, island=1, col=2)
    other = exchange(mine, col=1)

    part = pl.pallas_call(
        own_right_kernel,
        out_shape=jax.ShapeDtypeStruct((4, count, width), f32),
        in_specs=in_vmem(2),
        out_specs=in_vmem(1)[0],
        compiler_params=grant(8),
        cost_estimate=work(2 * rows // 2 * cols * count),
        name="own_right",
    )(kept, mine)
    block0, block1, block2, block3 = pl.pallas_call(
        right_kernel,
        out_shape=(long_shape, long_shape, block_shape, block_shape),
        in_specs=in_vmem(4),
        out_specs=in_vmem(4),
        compiler_params=grant(8),
        name="right",
    )(kept, mine, other, part)
    summed = pl.pallas_call(add_kernel, out_shape=long_shape, in_specs=in_vmem(4), out_specs=in_vmem(1)[0], compiler_params=grant(2), name="add")(
        block0, exchange(block1, row=1), exchange(block2, island=1), exchange(block3, island=1, row=1)
    )
    total, gram = pl.pallas_call(
        finish_kernel,
        out_shape=(block_shape, jax.ShapeDtypeStruct((extra, width), f32)),
        in_specs=in_vmem(2),
        out_specs=in_vmem(2),
        compiler_params=grant(2),
        name="finish",
    )(summed, exchange(summed, row=2))
    rights = [total, exchange(total, row=1), exchange(total, island=1), exchange(total, island=1, row=1)]
    left = pl.pallas_call(
        inverse_kernel,
        out_shape=jax.ShapeDtypeStruct((rows, 3 * count), jnp.bfloat16),
        in_specs=in_vmem(3),
        out_specs=in_vmem(1)[0],
        scratch_shapes=[pltpu.VMEM((count, rows), f32)],
        cost_estimate=work(6 * rows * cols * count),
        compiler_params=grant(6),
        name="inverse",
    )(gram, mine, other)
    updated = pl.pallas_call(
        update_kernel,
        out_shape=jax.ShapeDtypeStruct((rows, cols), f32),
        in_specs=in_vmem(6),
        out_specs=anywhere,
        scratch_shapes=[pltpu.VMEM((4, rows, width), f32), pltpu.SemaphoreType.DMA((4,))],
        compiler_params=grant(14),
        name="update",
    )(kept, left, *rights)
    return updated[None]


def solution(mesh):
    in_specs = (P("island", "row", "col"), P(None, None, "col"), P())
    out_specs = P("island", "row", "col")
    sizes = tuple(mesh.shape[axis] for axis in AXES)
    body = two_islands if sizes == (2, 4, 4) else any_islands
    return jax.shard_map(body, mesh=mesh, in_specs=in_specs, out_specs=out_specs, check_vma=False)
```

```python
import jax
import jax.numpy as jnp
from jax import lax
from jax.experimental import pallas as pl
from jax.experimental.pallas import tpu as pltpu
from jax.sharding import PartitionSpec as P

MATCHINGS = 2
AXES = ("island", "row", "col")


def partner_list(pair_rows, islands):
    positions = jnp.arange(islands, dtype=jnp.int32)
    first = pair_rows[:, 0]
    second = pair_rows[:, 1]
    from_first = jnp.where(first[None, :] == positions[:, None], second[None, :], 0)
    from_second = jnp.where(second[None, :] == positions[:, None], first[None, :], 0)
    return jnp.sum(from_first + from_second, axis=1)


def orthonormal(gram_matrix, left_factor):
    lower_factor = jnp.linalg.cholesky(gram_matrix)
    return jax.scipy.linalg.solve_triangular(lower_factor, left_factor, lower=True)


def combine_partner(values, partner_row, myself, factor_sign):
    islands = lax.axis_size("island")
    gathered = lax.all_gather(values[None], "island", axis=0, tiled=True)
    positions = jnp.arange(islands, dtype=jnp.int32)
    mine = jnp.sum(jnp.where(positions == myself, partner_row, 0))
    partner_term = lax.dynamic_index_in_dim(gathered, mine, 0, keepdims=False)
    return values + factor_sign * partner_term


def any_islands(weights, bases, pairs):
    myself = lax.axis_index("island")
    islands = lax.axis_size("island")
    weight_tile = weights[0]
    for matching in range(MATCHINGS):
        base_rows = bases[matching]
        partner_row = partner_list(pairs[matching], islands)
        partial_terms = lax.dot_general(
            base_rows,
            weight_tile,
            (((1,), (1,)), ((), ())),
            precision=lax.Precision.HIGHEST,
            preferred_element_type=jnp.float32,
        )
        left_terms = lax.psum(partial_terms, "col")
        left_factor = combine_partner(left_terms, partner_row, myself, -1.0)
        local_gram = jnp.dot(left_factor, left_factor.T, precision=lax.Precision.HIGHEST)
        gram_matrix = lax.psum(local_gram, "row")
        left_basis = orthonormal(gram_matrix, left_factor)
        right_partial = jnp.dot(left_basis, weight_tile, precision=lax.Precision.HIGHEST)
        right_terms = lax.psum(right_partial, "row")
        right_factor = combine_partner(right_terms, partner_row, myself, 1.0)
        correction = lax.dot_general(
            left_basis,
            right_factor,
            (((0,), (0,)), ((), ())),
            precision=lax.Precision.HIGHEST,
            preferred_element_type=jnp.float32,
        )
        weight_tile = weight_tile - 0.5 * correction
    return weight_tile[None]


def exchange(values, island=0, row=0, col=0):
    sizes = [lax.axis_size(axis) for axis in AXES]
    pairs = []
    for i in range(sizes[0]):
        for r in range(sizes[1]):
            for c in range(sizes[2]):
                here = (i * sizes[1] + r) * sizes[2] + c
                there = ((i ^ island) * sizes[1] + (r ^ row)) * sizes[2] + (c ^ col)
                pairs.append((here, there))
    return lax.ppermute(values, AXES, pairs)


def split(values):
    high = values.astype(jnp.bfloat16)
    return high, (values - high.astype(jnp.float32)).astype(jnp.bfloat16)


def matmul(left, right, contract):
    return lax.dot_general(left, right, (contract, ((), ())), preferred_element_type=jnp.float32)


def island_sign():
    return jnp.where(lax.axis_index("island") == 0, 1.0, -1.0).astype(jnp.float32)


def core_halves(rows):
    core = lax.rem(lax.axis_index("col"), 2)
    half = rows // 2
    return pl.multiple_of(core * half, half), pl.multiple_of((1 - core) * half, half)


def half_copies(tile_ref, kept_ref, sems, start):
    size = kept_ref.shape[0] // sems.shape[0]
    spans = [pl.ds(block * size, size) for block in range(sems.shape[0])]
    sources = [pl.ds(pl.multiple_of(start + block * size, size), size) for block in range(sems.shape[0])]
    copies = [pltpu.make_async_copy(tile_ref.at[source, :], kept_ref.at[span, :], sems.at[i]) for i, (source, span) in enumerate(zip(sources, spans))]
    return spans, copies


def left_rows(tile, both):
    size = tile.shape[0]
    products = matmul(jnp.concatenate(split(tile), axis=0), both, ((1,), (0,)))
    turned = (products[:size] + products[size:]).T
    count = turned.shape[0] // 2
    return turned[:count] + turned[count:]


def left_kernel(tile_ref, bases_ref, kept_ref, later_ref, out_ref, both_ref, rows_buffer, rows_sem, sems, later_sems):
    rows, cols = tile_ref.shape
    mine, other = core_halves(rows)
    rows_copy = pltpu.make_async_copy(bases_ref, rows_buffer, rows_sem)
    rows_copy.start()
    spans, copies = half_copies(tile_ref, kept_ref, sems, other)
    _, later_copies = half_copies(tile_ref, later_ref, later_sems, mine)
    for copy in copies + later_copies:
        copy.start()
    rows_copy.wait()
    stacked = rows_buffer[...].reshape(-1, cols) * island_sign()
    both = jnp.concatenate([part.astype(jnp.float32) for part in split(stacked)], axis=0).T.astype(jnp.bfloat16)
    both_ref[...] = both
    for span, copy in zip(spans, copies):
        copy.wait()
        out_ref[:, span] = left_rows(kept_ref[span, :], both)
    for copy in later_copies:
        copy.wait()


def rest_kernel(kept_ref, both_ref, out_ref):
    size = kept_ref.shape[0] // 2
    both = both_ref[...]
    for block in range(2):
        span = pl.ds(block * size, size)
        out_ref[:, span] = left_rows(kept_ref[span, :], both)


def block_spans(width):
    place = lax.axis_index("island") * 2 + lax.rem(lax.axis_index("row"), 2)
    return [pl.ds(pl.multiple_of(lax.bitwise_xor(place, k) * width, width), width) for k in range(4)]


def gram_of(values):
    return lax.dot_general(values, values, (((1,), (1,)), ((), ())), precision=lax.Precision.HIGHEST, preferred_element_type=jnp.float32)


def right_block(tile, both, high):
    count = high.shape[0]
    tile_high, tile_low = split(tile)
    first = matmul(both, tile_high, ((1,), (0,)))
    second = matmul(high, tile_low, ((1,), (0,)))
    return first[:count] + first[count:] + second


def own_right_kernel(kept_ref, mine_ref, out_ref, gram_ref):
    values = mine_ref[...]
    gram_ref[...] = gram_of(values)
    high, low = split(values * island_sign())
    both = jnp.concatenate([high, low], axis=0)
    for block, span in enumerate(block_spans(kept_ref.shape[1] // 4)):
        out_ref[block] = right_block(kept_ref[:, span], both, high)


def right_kernel(kept_ref, other_ref, part_ref, gram_ref, out0_ref, out1_ref, out2_ref, out3_ref):
    values = other_ref[...]
    count = values.shape[0]
    gram = gram_ref[...] + gram_of(values)
    quarter = count // 4
    packed = jnp.concatenate([gram[i * quarter : (i + 1) * quarter, :] for i in range(4)], axis=1)
    out0_ref[count:, :] = packed
    out1_ref[count:, :] = packed
    high, low = split(values * island_sign())
    both = jnp.concatenate([high, low], axis=0)
    outs = (out0_ref, out1_ref, out2_ref, out3_ref)
    for block, span in enumerate(block_spans(kept_ref.shape[1] // 4)):
        outs[block][:count, :] = part_ref[block] + right_block(kept_ref[:, span], both, high)


def add_kernel(own_ref, near_ref, across_ref, both_ref, out_ref):
    count = across_ref.shape[0]
    out_ref[:count, :] = own_ref[:count, :] + near_ref[:count, :] + across_ref[...] + both_ref[...]
    out_ref[count:, :] = own_ref[count:, :] + near_ref[count:, :]


def finish_kernel(own_ref, far_ref, total_ref, gram_ref):
    count = total_ref.shape[0]
    total_ref[...] = own_ref[:count, :] + far_ref[:count, :]
    gram_ref[...] = own_ref[count:, :] + far_ref[count:, :]


def inverse_kernel(packed_ref, mine_ref, other_ref, out_ref):
    packed = packed_ref[...]
    quarter = packed.shape[0]
    count = 4 * quarter
    matrix = jnp.concatenate([packed[:, i * count : (i + 1) * count] for i in range(4)], axis=0)
    row_index = lax.broadcasted_iota(jnp.int32, (count, count), 0)
    col_index = lax.broadcasted_iota(jnp.int32, (count, count), 1)
    panel = 8
    for first in range(0, count, panel):
        columns = [jnp.broadcast_to(matrix[:, first + k : first + k + 1], (count, count)) for k in range(panel)]
        for k in range(panel):
            pivot = first + k
            inverse = 1.0 / columns[k][pivot : pivot + 1, :]
            scaled = matrix[pivot : pivot + 1, :] * inverse
            in_row = row_index == pivot
            matrix = jnp.where(in_row, scaled, matrix - columns[k] * scaled)
            matrix = jnp.where(col_index == pivot, jnp.where(in_row, -inverse, columns[k] * inverse), matrix)
            for later in range(k + 1, panel):
                entry = columns[later][pivot : pivot + 1, :] * inverse
                columns[later] = jnp.where(in_row, entry, columns[later] - columns[k] * entry)
    scaled = matrix * (-0.5 * island_sign())
    for half, factor_ref in enumerate((mine_ref, other_ref)):
        values = lax.dot_general(scaled, factor_ref[...], (((0,), (0,)), ((), ())), precision=lax.Precision.HIGHEST, preferred_element_type=jnp.float32)
        high, low = split(values.T)
        out_ref[half] = jnp.concatenate([high, high, low], axis=1)


def update_kernel(mine_ref, other_ref, left_ref, right0_ref, right1_ref, right2_ref, right3_ref, out_ref, results, sems):
    half, cols = mine_ref.shape
    starts = core_halves(2 * half)
    spans = block_spans(cols // 4)
    stores = []
    for k, right_ref in enumerate((right0_ref, right1_ref, right2_ref, right3_ref)):
        high, low = split(right_ref[...])
        right = jnp.concatenate([high, low, high], axis=0)
        for part, kept_ref in enumerate((mine_ref, other_ref)):
            results[k, part] = kept_ref[:, spans[k]] - matmul(left_ref[part], right, ((1,), (0,)))
            store = pltpu.make_async_copy(results.at[k, part], out_ref.at[pl.ds(starts[part], half), spans[k]], sems.at[k, part])
            store.start()
            stores.append(store)
    for store in stores:
        store.wait()


def in_vmem(count):
    return [pl.BlockSpec(memory_space=pltpu.VMEM)] * count


def grant(mebibytes):
    return pltpu.CompilerParams(vmem_limit_bytes=mebibytes << 20)


def work(flops):
    return pl.CostEstimate(flops=flops, bytes_accessed=flops // 32, transcendentals=0)


def two_islands(weights, bases, pairs):
    del pairs
    tile = weights[0]
    rows, cols = tile.shape
    count = bases.shape[0] * bases.shape[1]
    width = cols // 4
    extra = count // 4
    f32 = jnp.float32
    anywhere = pl.BlockSpec(memory_space=pl.ANY)
    half_shape = jax.ShapeDtypeStruct((count, rows // 2), f32)
    block_shape = jax.ShapeDtypeStruct((count, width), f32)
    long_shape = jax.ShapeDtypeStruct((count + extra, width), f32)

    hbm_tile, hbm_bases = (pltpu.with_memory_space_constraint(array, pltpu.HBM) for array in (tile, bases))
    half_tile = jax.ShapeDtypeStruct((rows // 2, cols), f32)
    kept_other, kept_mine, other, both = pl.pallas_call(
        left_kernel,
        out_shape=(half_tile, half_tile, half_shape, jax.ShapeDtypeStruct((cols, 2 * count), jnp.bfloat16)),
        in_specs=[anywhere] * 2,
        out_specs=in_vmem(4),
        scratch_shapes=[pltpu.VMEM(bases.shape, f32), pltpu.SemaphoreType.DMA(()), pltpu.SemaphoreType.DMA((1,)), pltpu.SemaphoreType.DMA((1,))],
        compiler_params=grant(8),
        name="left",
    )(hbm_tile, hbm_bases)
    crossed = exchange(other, col=1)
    mine = pl.pallas_call(
        rest_kernel,
        out_shape=half_shape,
        in_specs=in_vmem(2),
        out_specs=in_vmem(1)[0],
        compiler_params=grant(6),
        cost_estimate=work(2 * rows // 2 * cols * count),
        name="rest",
    )(kept_mine, both)
    mine = mine + crossed
    mine = mine + exchange(mine, island=1) + exchange(mine, col=2) + exchange(mine, island=1, col=2)
    other = exchange(mine, col=1)

    part, own_gram = pl.pallas_call(
        own_right_kernel,
        out_shape=(jax.ShapeDtypeStruct((4, count, width), f32), jax.ShapeDtypeStruct((count, count), f32)),
        in_specs=in_vmem(2),
        out_specs=in_vmem(2),
        compiler_params=grant(8),
        cost_estimate=work(2 * rows // 2 * cols * count),
        name="own_right",
    )(kept_mine, mine)
    block0, block1, block2, block3 = pl.pallas_call(
        right_kernel,
        out_shape=(long_shape, long_shape, block_shape, block_shape),
        in_specs=in_vmem(4),
        out_specs=in_vmem(4),
        compiler_params=grant(8),
        name="right",
    )(kept_other, other, part, own_gram)
    summed = pl.pallas_call(add_kernel, out_shape=long_shape, in_specs=in_vmem(4), out_specs=in_vmem(1)[0], compiler_params=grant(2), name="add")(
        block0, exchange(block1, row=1), exchange(block2, island=1), exchange(block3, island=1, row=1)
    )
    total, gram = pl.pallas_call(
        finish_kernel,
        out_shape=(block_shape, jax.ShapeDtypeStruct((extra, width), f32)),
        in_specs=in_vmem(2),
        out_specs=in_vmem(2),
        compiler_params=grant(2),
        name="finish",
    )(summed, exchange(summed, row=2))
    rights = [total, exchange(total, row=1), exchange(total, island=1), exchange(total, island=1, row=1)]
    left = pl.pallas_call(
        inverse_kernel,
        out_shape=jax.ShapeDtypeStruct((2, rows // 2, 3 * count), jnp.bfloat16),
        in_specs=in_vmem(3),
        out_specs=in_vmem(1)[0],
        cost_estimate=work(6 * rows * cols * count),
        compiler_params=grant(6),
        name="inverse",
    )(gram, mine, other)
    updated = pl.pallas_call(
        update_kernel,
        out_shape=jax.ShapeDtypeStruct((rows, cols), f32),
        in_specs=in_vmem(7),
        out_specs=anywhere,
        scratch_shapes=[pltpu.VMEM((4, 2, rows // 2, width), f32), pltpu.SemaphoreType.DMA((4, 2))],
        compiler_params=grant(14),
        name="update",
    )(kept_mine, kept_other, left, *rights)
    return updated[None]


def solution(mesh):
    in_specs = (P("island", "row", "col"), P(None, None, "col"), P())
    out_specs = P("island", "row", "col")
    sizes = tuple(mesh.shape[axis] for axis in AXES)
    body = two_islands if sizes == (2, 4, 4) else any_islands
    return jax.shard_map(body, mesh=mesh, in_specs=in_specs, out_specs=out_specs, check_vma=False)
```

```python
import jax
import jax.numpy as jnp
from jax import lax
from jax.experimental import pallas as pl
from jax.experimental.pallas import tpu as pltpu
from jax.sharding import PartitionSpec as P

MATCHINGS = 2
AXES = ("island", "row", "col")


def partner_list(pair_rows, islands):
    positions = jnp.arange(islands, dtype=jnp.int32)
    first = pair_rows[:, 0]
    second = pair_rows[:, 1]
    from_first = jnp.where(first[None, :] == positions[:, None], second[None, :], 0)
    from_second = jnp.where(second[None, :] == positions[:, None], first[None, :], 0)
    return jnp.sum(from_first + from_second, axis=1)


def orthonormal(gram_matrix, left_factor):
    lower_factor = jnp.linalg.cholesky(gram_matrix)
    return jax.scipy.linalg.solve_triangular(lower_factor, left_factor, lower=True)


def combine_partner(values, partner_row, myself, factor_sign):
    islands = lax.axis_size("island")
    gathered = lax.all_gather(values[None], "island", axis=0, tiled=True)
    positions = jnp.arange(islands, dtype=jnp.int32)
    mine = jnp.sum(jnp.where(positions == myself, partner_row, 0))
    partner_term = lax.dynamic_index_in_dim(gathered, mine, 0, keepdims=False)
    return values + factor_sign * partner_term


def any_islands(weights, bases, pairs):
    myself = lax.axis_index("island")
    islands = lax.axis_size("island")
    weight_tile = weights[0]
    for matching in range(MATCHINGS):
        base_rows = bases[matching]
        partner_row = partner_list(pairs[matching], islands)
        partial_terms = lax.dot_general(
            base_rows,
            weight_tile,
            (((1,), (1,)), ((), ())),
            precision=lax.Precision.HIGHEST,
            preferred_element_type=jnp.float32,
        )
        left_terms = lax.psum(partial_terms, "col")
        left_factor = combine_partner(left_terms, partner_row, myself, -1.0)
        local_gram = jnp.dot(left_factor, left_factor.T, precision=lax.Precision.HIGHEST)
        gram_matrix = lax.psum(local_gram, "row")
        left_basis = orthonormal(gram_matrix, left_factor)
        right_partial = jnp.dot(left_basis, weight_tile, precision=lax.Precision.HIGHEST)
        right_terms = lax.psum(right_partial, "row")
        right_factor = combine_partner(right_terms, partner_row, myself, 1.0)
        correction = lax.dot_general(
            left_basis,
            right_factor,
            (((0,), (0,)), ((), ())),
            precision=lax.Precision.HIGHEST,
            preferred_element_type=jnp.float32,
        )
        weight_tile = weight_tile - 0.5 * correction
    return weight_tile[None]


def exchange(values, island=0, row=0, col=0):
    sizes = [lax.axis_size(axis) for axis in AXES]
    pairs = []
    for i in range(sizes[0]):
        for r in range(sizes[1]):
            for c in range(sizes[2]):
                here = (i * sizes[1] + r) * sizes[2] + c
                there = ((i ^ island) * sizes[1] + (r ^ row)) * sizes[2] + (c ^ col)
                pairs.append((here, there))
    return lax.ppermute(values, AXES, pairs)


def split(values):
    high = values.astype(jnp.bfloat16)
    return high, (values - high.astype(jnp.float32)).astype(jnp.bfloat16)


def matmul(left, right, contract):
    return lax.dot_general(left, right, (contract, ((), ())), preferred_element_type=jnp.float32)


def island_sign():
    return jnp.where(lax.axis_index("island") == 0, 1.0, -1.0).astype(jnp.float32)


def core_halves(rows):
    core = lax.rem(lax.axis_index("col"), 2)
    half = rows // 2
    return pl.multiple_of(core * half, half), pl.multiple_of((1 - core) * half, half)


def half_copies(tile_ref, kept_ref, sems, start):
    size = kept_ref.shape[0] // sems.shape[0]
    spans = [pl.ds(block * size, size) for block in range(sems.shape[0])]
    sources = [pl.ds(pl.multiple_of(start + block * size, size), size) for block in range(sems.shape[0])]
    copies = [pltpu.make_async_copy(tile_ref.at[source, :], kept_ref.at[span, :], sems.at[i]) for i, (source, span) in enumerate(zip(sources, spans))]
    return spans, copies


def left_rows(tile, both):
    size = tile.shape[0]
    products = matmul(jnp.concatenate(split(tile), axis=0), both, ((1,), (0,)))
    turned = (products[:size] + products[size:]).T
    count = turned.shape[0] // 2
    return turned[:count] + turned[count:]


def left_kernel(tile_ref, bases_ref, kept_ref, later_ref, out_ref, both_ref, rows_buffer, rows_sem, sems, later_sems):
    rows, cols = tile_ref.shape
    mine, other = core_halves(rows)
    rows_copy = pltpu.make_async_copy(bases_ref, rows_buffer, rows_sem)
    rows_copy.start()
    spans, copies = half_copies(tile_ref, kept_ref, sems, other)
    _, later_copies = half_copies(tile_ref, later_ref, later_sems, mine)
    for copy in copies + later_copies:
        copy.start()
    rows_copy.wait()
    stacked = rows_buffer[...].reshape(-1, cols) * island_sign()
    both = jnp.concatenate([part.astype(jnp.float32) for part in split(stacked)], axis=0).T.astype(jnp.bfloat16)
    both_ref[...] = both
    for span, copy in zip(spans, copies):
        copy.wait()
        out_ref[:, span] = left_rows(kept_ref[span, :], both)
    for copy in later_copies:
        copy.wait()


def rest_kernel(kept_ref, both_ref, out_ref):
    size = kept_ref.shape[0] // 2
    both = both_ref[...]
    for block in range(2):
        span = pl.ds(block * size, size)
        out_ref[:, span] = left_rows(kept_ref[span, :], both)


def block_spans(width):
    place = lax.axis_index("island") * 2 + lax.rem(lax.axis_index("row"), 2)
    return [pl.ds(pl.multiple_of(lax.bitwise_xor(place, k) * width, width), width) for k in range(4)]


def gram_of(values):
    return lax.dot_general(values, values, (((1,), (1,)), ((), ())), precision=lax.Precision.HIGHEST, preferred_element_type=jnp.float32)


def right_block(tile, both, high):
    count = high.shape[0]
    tile_high, tile_low = split(tile)
    first = matmul(both, tile_high, ((1,), (0,)))
    second = matmul(high, tile_low, ((1,), (0,)))
    return first[:count] + first[count:] + second


def own_right_kernel(kept_ref, mine_ref, out_ref, gram_ref):
    values = mine_ref[...]
    gram_ref[...] = gram_of(values)
    high, low = split(values * island_sign())
    both = jnp.concatenate([high, low], axis=0)
    for block, span in enumerate(block_spans(kept_ref.shape[1] // 4)):
        out_ref[block] = right_block(kept_ref[:, span], both, high)


def right_kernel(kept_ref, other_ref, part_ref, gram_ref, out0_ref, out1_ref, out2_ref, out3_ref):
    values = other_ref[...]
    count = values.shape[0]
    gram = gram_ref[...] + gram_of(values)
    quarter = count // 4
    packed = jnp.concatenate([gram[i * quarter : (i + 1) * quarter, :] for i in range(4)], axis=1)
    out0_ref[count:, :] = packed
    out1_ref[count:, :] = packed
    high, low = split(values * island_sign())
    both = jnp.concatenate([high, low], axis=0)
    outs = (out0_ref, out1_ref, out2_ref, out3_ref)
    for block, span in enumerate(block_spans(kept_ref.shape[1] // 4)):
        outs[block][:count, :] = part_ref[block] + right_block(kept_ref[:, span], both, high)


def add_kernel(own_ref, near_ref, across_ref, both_ref, out_ref):
    count = across_ref.shape[0]
    out_ref[:count, :] = own_ref[:count, :] + near_ref[:count, :] + across_ref[...] + both_ref[...]
    out_ref[count:, :] = own_ref[count:, :] + near_ref[count:, :]


def finish_kernel(own_ref, far_ref, total_ref, gram_ref):
    count = total_ref.shape[0]
    total_ref[...] = own_ref[:count, :] + far_ref[:count, :]
    gram_ref[...] = own_ref[count:, :] + far_ref[count:, :]


def inverse_kernel(packed_ref, mine_ref, other_ref, out_ref):
    packed = packed_ref[...]
    quarter = packed.shape[0]
    count = 4 * quarter
    matrix = jnp.concatenate([packed[:, i * count : (i + 1) * count] for i in range(4)], axis=0)
    row_index = lax.broadcasted_iota(jnp.int32, (count, count), 0)
    col_index = lax.broadcasted_iota(jnp.int32, (count, count), 1)
    lane = lax.broadcasted_iota(jnp.int32, (1, count), 1)
    panel = 8
    for first in range(0, count, panel):
        columns = [jnp.broadcast_to(matrix[:, first + k : first + k + 1], (count, count)) for k in range(panel)]
        matrix = jnp.where((col_index >= first) & (col_index < first + panel), 0.0, matrix)
        for k in range(panel):
            pivot = first + k
            inverse = 1.0 / columns[k][pivot : pivot + 1, :]
            scaled = jnp.where(lane == pivot, -inverse, matrix[pivot : pivot + 1, :] * inverse)
            in_row = row_index == pivot
            matrix = jnp.where(in_row, scaled, matrix - columns[k] * scaled)
            for later in range(k + 1, panel):
                entry = columns[later][pivot : pivot + 1, :] * inverse
                columns[later] = jnp.where(in_row, entry, columns[later] - columns[k] * entry)
    scaled = matrix * (-0.5 * island_sign())
    for half, factor_ref in enumerate((mine_ref, other_ref)):
        values = lax.dot_general(scaled, factor_ref[...], (((0,), (0,)), ((), ())), precision=lax.Precision.HIGHEST, preferred_element_type=jnp.float32)
        high, low = split(values.T)
        out_ref[half] = jnp.concatenate([high, high, low], axis=1)


def update_kernel(mine_ref, other_ref, left_ref, right0_ref, right1_ref, right2_ref, right3_ref, out_ref, results, sems):
    half, cols = mine_ref.shape
    starts = core_halves(2 * half)
    spans = block_spans(cols // 4)
    stores = []
    for k, right_ref in enumerate((right0_ref, right1_ref, right2_ref, right3_ref)):
        high, low = split(right_ref[...])
        right = jnp.concatenate([high, low, high], axis=0)
        for part, kept_ref in enumerate((mine_ref, other_ref)):
            results[k, part] = kept_ref[:, spans[k]] - matmul(left_ref[part], right, ((1,), (0,)))
            store = pltpu.make_async_copy(results.at[k, part], out_ref.at[pl.ds(starts[part], half), spans[k]], sems.at[k, part])
            store.start()
            stores.append(store)
    for store in stores:
        store.wait()


def in_vmem(count):
    return [pl.BlockSpec(memory_space=pltpu.VMEM)] * count


def grant(mebibytes):
    return pltpu.CompilerParams(vmem_limit_bytes=mebibytes << 20)


def work(flops):
    return pl.CostEstimate(flops=flops, bytes_accessed=flops // 32, transcendentals=0)


def two_islands(weights, bases, pairs):
    del pairs
    tile = weights[0]
    rows, cols = tile.shape
    count = bases.shape[0] * bases.shape[1]
    width = cols // 4
    extra = count // 4
    f32 = jnp.float32
    anywhere = pl.BlockSpec(memory_space=pl.ANY)
    half_shape = jax.ShapeDtypeStruct((count, rows // 2), f32)
    block_shape = jax.ShapeDtypeStruct((count, width), f32)
    long_shape = jax.ShapeDtypeStruct((count + extra, width), f32)

    hbm_tile, hbm_bases = (pltpu.with_memory_space_constraint(array, pltpu.HBM) for array in (tile, bases))
    half_tile = jax.ShapeDtypeStruct((rows // 2, cols), f32)
    kept_other, kept_mine, other, both = pl.pallas_call(
        left_kernel,
        out_shape=(half_tile, half_tile, half_shape, jax.ShapeDtypeStruct((cols, 2 * count), jnp.bfloat16)),
        in_specs=[anywhere] * 2,
        out_specs=in_vmem(4),
        scratch_shapes=[pltpu.VMEM(bases.shape, f32), pltpu.SemaphoreType.DMA(()), pltpu.SemaphoreType.DMA((1,)), pltpu.SemaphoreType.DMA((1,))],
        compiler_params=grant(8),
        name="left",
    )(hbm_tile, hbm_bases)
    crossed = exchange(other, col=1)
    mine = pl.pallas_call(
        rest_kernel,
        out_shape=half_shape,
        in_specs=in_vmem(2),
        out_specs=in_vmem(1)[0],
        compiler_params=grant(6),
        cost_estimate=work(2 * rows // 2 * cols * count),
        name="rest",
    )(kept_mine, both)
    mine = mine + crossed
    mine = mine + exchange(mine, island=1) + exchange(mine, col=2) + exchange(mine, island=1, col=2)
    other = exchange(mine, col=1)

    part, own_gram = pl.pallas_call(
        own_right_kernel,
        out_shape=(jax.ShapeDtypeStruct((4, count, width), f32), jax.ShapeDtypeStruct((count, count), f32)),
        in_specs=in_vmem(2),
        out_specs=in_vmem(2),
        compiler_params=grant(8),
        cost_estimate=work(2 * rows // 2 * cols * count),
        name="own_right",
    )(kept_mine, mine)
    block0, block1, block2, block3 = pl.pallas_call(
        right_kernel,
        out_shape=(long_shape, long_shape, block_shape, block_shape),
        in_specs=in_vmem(4),
        out_specs=in_vmem(4),
        compiler_params=grant(8),
        name="right",
    )(kept_other, other, part, own_gram)
    summed = pl.pallas_call(add_kernel, out_shape=long_shape, in_specs=in_vmem(4), out_specs=in_vmem(1)[0], compiler_params=grant(2), name="add")(
        block0, exchange(block1, row=1), exchange(block2, island=1), exchange(block3, island=1, row=1)
    )
    total, gram = pl.pallas_call(
        finish_kernel,
        out_shape=(block_shape, jax.ShapeDtypeStruct((extra, width), f32)),
        in_specs=in_vmem(2),
        out_specs=in_vmem(2),
        compiler_params=grant(2),
        name="finish",
    )(summed, exchange(summed, row=2))
    rights = [total, exchange(total, row=1), exchange(total, island=1), exchange(total, island=1, row=1)]
    left = pl.pallas_call(
        inverse_kernel,
        out_shape=jax.ShapeDtypeStruct((2, rows // 2, 3 * count), jnp.bfloat16),
        in_specs=in_vmem(3),
        out_specs=in_vmem(1)[0],
        cost_estimate=work(6 * rows * cols * count),
        compiler_params=grant(6),
        name="inverse",
    )(gram, mine, other)
    updated = pl.pallas_call(
        update_kernel,
        out_shape=jax.ShapeDtypeStruct((rows, cols), f32),
        in_specs=in_vmem(7),
        out_specs=anywhere,
        scratch_shapes=[pltpu.VMEM((4, 2, rows // 2, width), f32), pltpu.SemaphoreType.DMA((4, 2))],
        compiler_params=grant(14),
        name="update",
    )(kept_mine, kept_other, left, *rights)
    return updated[None]


def solution(mesh):
    in_specs = (P("island", "row", "col"), P(None, None, "col"), P())
    out_specs = P("island", "row", "col")
    sizes = tuple(mesh.shape[axis] for axis in AXES)
    body = two_islands if sizes == (2, 4, 4) else any_islands
    if body is any_islands:
        return jax.shard_map(body, mesh=mesh, in_specs=in_specs, out_specs=out_specs, check_vma=False)

    return jax.shard_map(body, mesh=mesh, in_specs=in_specs, out_specs=out_specs, check_vma=False)
```
